32 devices in a mesh: dp: 4 (over x, core), fsdp: 8 (over z, y).
Axes of the slice: x: 2, y: 2, z: 4, core: 2. Of those that a mesh axis runs over, the one named last changes fastest.
Arguments:
- tokens: bfloat16 [64, 512, 768], P(('dp', 'fsdp')), may hold values from -6 to 6
- segment_ids: int32 [64, 512], P(('dp', 'fsdp')), may hold values from 0 to 32, as said below
- qkv_weight: bfloat16 [768, 576], P(('dp', 'fsdp')), may hold values from -0.4375 to 0.4375
- out_weight: bfloat16 [768, 768], P(('dp', 'fsdp')), may hold values from -2.5 to 2.5
- up_weight: bfloat16 [768, 768], P(('dp', 'fsdp')), may hold values from -0.4375 to 0.4375
- down_weight: bfloat16 [3072, 192], P(('dp', 'fsdp')), may hold values from -0.21875 to 0.21875
- biases: bfloat16 [6, 768], P(None, ('dp', 'fsdp')), may hold values from -1 to 1
- up_bias: bfloat16 [3072], P(('dp', 'fsdp')), may hold values from -2.5 to 2.5
- gains: bfloat16 [2, 768], P(None, ('dp', 'fsdp')), may hold values from 0.5 to 1.5
- cotangent: bfloat16 [64, 512, 768], P(('dp', 'fsdp')), may hold values from -6 to 6
Outputs:
- layer_out: bfloat16 [64, 512, 768], P(('dp', 'fsdp'))
- input_grad: float32 [64, 512, 768], P(('dp', 'fsdp'))
- qkv_grad: float32 [768, 576], P(('dp', 'fsdp'))
- out_grad: float32 [768, 768], P(('dp', 'fsdp'))
- up_grad: float32 [768, 768], P(('dp', 'fsdp'))
- down_grad: float32 [3072, 192], P(('dp', 'fsdp'))
- bias_grad: float32 [6, 768], P(None, ('dp', 'fsdp'))
- up_bias_grad: float32 [3072], P(('dp', 'fsdp'))
- gain_grad: float32 [2, 768], P(None, ('dp', 'fsdp'))
The draws below stay inside these ranges and needn't reach their ends.
Inputs may be any that keep to these rules, and one draw needn't show every extreme that they name: `segment_ids`: in each row the real tokens carry document numbers from 1 upward that never fall, each document contiguous; after them come 0 to 64 padding tokens numbered 0, exactly 64 in the first row.
All inputs are finite; a program needn't handle non-finite values.
Results may differ from the reference program's by a relative error of at most 0.012.
The reference program's roundings to bfloat16 on the way count: a program that leaves them out, or rounds other values in their place, can miss the bound.
Values may be sent and summed in bfloat16 or wider, within the bound.
A program may use at most 128 MiB of HBM per device.

```python
import math
import jax
import jax.numpy as jnp
from jax import lax

D = 768
HEADS = 12
FF = 3072
GROUPS = 4
L = 512
SEQS = 64
GW = 192
FFG = 768


def draw_segment_ids(key, part):
    first, second = jax.random.split(jax.random.fold_in(key, 7))
    position = jnp.arange(L, dtype=jnp.int32)[None, :]
    starts = (jax.random.randint(first, (SEQS, L), 0, 192) == 0).astype(jnp.int32)
    row_index = jnp.arange(SEQS, dtype=jnp.int32)[:, None]
    regular = (position % 8 == 0).astype(jnp.int32)
    starts = jnp.where(row_index == 0, regular, starts)
    starts = starts * (position > 0).astype(jnp.int32)
    numbers = jnp.minimum(1 + jnp.cumsum(starts, axis=1), L // 16)
    padding = jax.random.randint(second, (SEQS, 1), 0, L // 8 + 1)
    padding = padding.at[0, 0].set(L // 8)
    return jnp.where(position < L - padding, numbers, 0).astype(jnp.int32)


def with_spikes(drawn, rng, source, target, blocks, factor):
    owner, partner = [(jnp.arange(drawn.shape[dim]) // (drawn.shape[dim] // blocks)).reshape([-1 if axis == dim else 1 for axis in range(drawn.ndim)]) for dim in (source, target)]
    chosen = jax.random.permutation(rng, blocks)[partner]
    strong = (owner == chosen) | (owner == (partner + blocks // 2) % blocks)
    return jnp.where(strong, factor * drawn, drawn)


def shard_levels(rng, shape, cuts, least, high):
    factor_of = 1.0
    for dim, shards_of in cuts:
        draws = jax.random.uniform(jax.random.fold_in(jax.random.fold_in(rng, 6), dim), (shards_of,), jnp.float32, least / len(cuts), high / len(cuts))
        factor_of = factor_of * jnp.repeat(jnp.exp(draws), shape[dim] // shards_of).reshape((-1,) + (1,) * (len(shape) - 1 - dim))
    return factor_of


def normal_values(rng, dims, deviation, limit, cuts=(), kind=jnp.bfloat16):
    loudness = shard_levels(rng, dims, cuts, -0.22, 0.18) if cuts else 1.0
    values = jax.random.normal(rng, dims, jnp.float32) * deviation * loudness
    return jnp.minimum(jnp.maximum(values, -limit), limit).astype(kind)


def gaussian_with(stream_key, shape, spread, most, pieces, heavy, kind=jnp.bfloat16):
    drawn = spread * jax.random.normal(stream_key, shape, jnp.float32)
    if pieces:
        drawn = drawn * shard_levels(stream_key, shape, pieces, -0.22, 0.18)
    return jnp.clip(with_spikes(drawn, jax.random.fold_in(stream_key, 3), *heavy), -most, most).astype(kind)


def setup_inputs(seed: int = 0) -> dict:
    seeds = jax.random.split(jax.random.key(seed), 11)
    tokens = normal_values(seeds[0], (SEQS, L, D), 1.0, 6.0, ((0, 32),))
    segment_ids = draw_segment_ids(jax.random.fold_in(seeds[10], 71), 0)
    qkv_weight = normal_values(seeds[2], (D, 3 * GW), GW ** -0.5, 0.4375, ((0, 32),))
    out_weight = normal_values(seeds[3], (D, D), (max(1, D // 128)) ** -0.5, 2.5, ((0, 32),))
    up_weight = normal_values(seeds[4], (D, FFG), GW ** -0.5, 0.4375, ((0, 32),))
    down_weight = normal_values(seeds[5], (FF, GW), FFG ** -0.5, 0.21875, ((0, 32),))
    biases = normal_values(seeds[6], (6, D), 0.2, 1.0, ((1, 32),))
    up_bias = normal_values(seeds[7], (FF,), 0.5, 2.5, ((0, 32),))
    gains = jnp.clip(1.0 + 0.1 * jax.random.normal(seeds[8], (2, D), jnp.float32), 0.5, 1.5).astype(jnp.bfloat16)
    cotangent = gaussian_with(seeds[9], (SEQS, L, D), 1.0, 6.0, ((0, 32),), (0, 2, 32, 2.75))
    return {"tokens": tokens, "segment_ids": segment_ids, "qkv_weight": qkv_weight, "out_weight": out_weight, "up_weight": up_weight, "down_weight": down_weight, "biases": biases, "up_bias": up_bias, "gains": gains, "cotangent": cotangent}


@jax.custom_vjp
def low(v):
    return lax.optimization_barrier(v.astype(jnp.bfloat16)).astype(jnp.float32)

@jax.custom_vjp
def low_back(v):
    return v

def low_keep(v):
    return (low(v), None)

def low_pass(kept, grad):
    return (grad,)

def back_keep(v):
    return (v, None)

def back_low(kept, grad):
    return (low(grad),)
low.defvjp(low_keep, low_pass)
low_back.defvjp(back_keep, back_low)
EPSILON = 1e-05
SCORE_SCALE = 0.125
NEG_FILL = -1e+30
HIGHEST = lax.Precision.HIGHEST

def grouped(values, weight):
    parts = values.reshape(values.shape[0], GROUPS, -1)
    table = weight.reshape(GROUPS, parts.shape[2], -1)
    return jnp.einsum('ngc,gce->nge', parts, table, precision=HIGHEST)

def normalize(hidden):
    centre = hidden - lax.optimization_barrier(jnp.mean(hidden, -1, keepdims=True))
    return centre * lax.rsqrt(lax.optimization_barrier(jnp.mean(centre * centre, -1, keepdims=True)) + EPSILON)

def forward(inputs, weights, seg_rows):
    qkv_weight, out_weight, up_weight, down_weight, biases, up_bias, gains = weights
    count, length, width = inputs.shape
    rows = count * length
    group_w = width // GROUPS
    flat = inputs.reshape(rows, width)
    mixed = grouped(flat, qkv_weight)
    queries = low(low_back(mixed[:, :, :group_w].reshape(rows, width) + biases[0]))
    keys_all = low(low_back(mixed[:, :, group_w:2 * group_w].reshape(rows, width)))
    values_all = low(low_back(mixed[:, :, 2 * group_w:].reshape(rows, width) + biases[1]))
    shape4 = (count, length, HEADS, width // HEADS)
    raw = jnp.einsum('bqhd,bkhd->bhqk', queries.reshape(shape4), keys_all.reshape(shape4), precision=HIGHEST) * SCORE_SCALE
    live = seg_rows != 0
    allowed = live[:, None, :] & ((seg_rows[:, :, None] == seg_rows[:, None, :]) | (seg_rows[:, :, None] == 0))
    scores = low_back(jnp.where(allowed[:, None], raw, NEG_FILL))
    probs = low(jax.nn.softmax(scores, axis=-1))
    context = jnp.einsum('bhqk,bkhd->bqhd', probs, values_all.reshape(shape4), precision=HIGHEST).reshape(rows, width)
    context = low(low_back(context))
    attn = low_back(jnp.dot(context, out_weight, precision=HIGHEST))
    hidden1 = flat + attn + biases[2]
    layer1 = normalize(hidden1) * gains[0] + biases[3]
    pre_act = grouped(low(layer1), up_weight).reshape(rows, -1) + up_bias
    activ = low(jax.nn.gelu(low_back(pre_act), approximate=False))
    branch = low_back(grouped(activ, down_weight).reshape(rows, width))
    hidden2 = layer1 + branch + biases[4]
    result = normalize(hidden2) * gains[1] + biases[5]
    return result.reshape(count, length, width)

def reference(tokens, segment_ids, qkv_weight, out_weight, up_weight, down_weight, biases, up_bias, gains, cotangent):
    weights = tuple((w.astype(jnp.float32) for w in (qkv_weight, out_weight, up_weight, down_weight, biases, up_bias, gains)))
    block = math.gcd(SEQS, max(1, 4096 // L))
    turns = SEQS // block
    inputs = tokens.astype(jnp.float32).reshape(turns, block, L, D)
    seg_all = segment_ids.reshape(turns, block, L)
    cot_all = cotangent.astype(jnp.float32).reshape(turns, block, L, D)

    def accumulate(carry, item):
        span_in, span_seg, span_cot = item
        result, pull = jax.vjp(lambda values, *params: forward(values, params, span_seg), span_in, *weights)
        grads = pull(span_cot)
        carry = tuple((held + new for held, new in zip(carry, grads[1:])))
        return (carry, (result, grads[0]))
    start = tuple((jnp.zeros_like(w) for w in weights))
    totals, (results, in_grads) = lax.scan(accumulate, start, (inputs, seg_all, cot_all))
    layer_out = results.reshape(SEQS, L, D).astype(jnp.bfloat16)
    input_grad = in_grads.reshape(SEQS, L, D)
    return (layer_out, input_grad, totals[0], totals[1], totals[2], totals[3], totals[4], totals[5], totals[6])
```

```python
from functools import partial

import jax
import jax.numpy as jnp
from jax import lax
from jax.experimental import pallas as pl
from jax.experimental.pallas import tpu as pltpu
from jax.sharding import PartitionSpec as P

HEADS = 12
GROUPS = 4
EPSILON = 1e-05
SCORE_SCALE = 0.125
FAR = -1e30
F32 = jnp.float32
BF16 = jnp.bfloat16
ERF_P = 0.39
ERF_C = (
    0.23532515472880694, 0.09138881837358971, 0.6495583919191722,
    -0.6353990321145604, 0.8866636029850097, -0.22753693758818713,
)
NT = (((1,), (1,)), ((), ()))
TN = (((0,), (0,)), ((), ()))


def dot(a, b):
    return jnp.dot(a, b, preferred_element_type=F32)


def dot_nt(a, b):
    return lax.dot_general(a, b, NT, preferred_element_type=F32)


def dot_tn(a, b):
    return lax.dot_general(a, b, TN, preferred_element_type=F32)


def edge(group):
    return (group // 2) * 384 + (group % 2) * 128


def inset(group):
    return (group % 2) * 64


def aligned(value, step):
    return value if isinstance(value, int) else pl.multiple_of(value, step)


def lane_ids(shape):
    return lax.broadcasted_iota(jnp.int32, shape, len(shape) - 1)


def head_only(block, head, extra=False):
    lanes = lane_ids(block.shape)
    keep = (lanes >= 64 * head) & (lanes < 64 * head + 64)
    if extra:
        keep = keep | (lanes >= 192)
    return jnp.where(keep, block, jnp.zeros_like(block))


def gelu_pair(v):
    a = jnp.abs(v)
    u = jnp.exp(v * v * (-0.5))
    t = 1.0 / (1.0 + a * (ERF_P * 0.7071067811865476))
    h = ERF_C[5] * 0.5
    for c in ERF_C[4::-1]:
        h = h * t + 0.5 * c
    h = h * t * u
    phi = jnp.where(v >= 0, 1.0 - h, h)
    return v * phi, phi + v * u * 0.3989422804014327


def normalize(hidden):
    centre = hidden - jnp.mean(hidden, -1, keepdims=True)
    spread = lax.rsqrt(jnp.mean(centre * centre, -1, keepdims=True) + EPSILON)
    return centre * spread, spread


def norm_back(upstream, gain, normed, spread):
    scaled = upstream * gain
    return spread * (
        scaled
        - jnp.mean(scaled, -1, keepdims=True)
        - normed * jnp.mean(scaled * normed, -1, keepdims=True)
    )


def spread_windows(parts):
    tiles = []
    for pair in range(2):
        low, high = parts[2 * pair], parts[2 * pair + 1]
        tiles += [low[:, :128], low[:, 128:] + high[:, :128], high[:, 128:]]
    return jnp.concatenate(tiles, -1)


def col_sum(v):
    return jnp.sum(v, 0, keepdims=True)


def body(
    x_ref, seg_ref, cot_ref, buf_a, buf_o, buf_u, buf_d,
    lo_ref, ig_ref, ga_ref, go_ref, gu_ref, gd_ref,
    piece, wqkv, wo, wup, wdn, small, rows_sm, upb,
    qext, kext, qs, kk, vv, ctx, gctx, gm, lse, lse_t,
    acc_o, acc_u, acc_d, acc_q, acc_b, acc_ub, acc_qv, tmp_t,
):
    count, length = seg_ref.shape
    rows, width = x_ref.shape
    n_dev, take, _ = buf_a.shape
    per = n_dev // GROUPS
    take_d = buf_d.shape[1]

    wqkv[...] = jnp.zeros_like(wqkv)
    wo[...] = jnp.zeros_like(wo)
    wup[...] = jnp.zeros_like(wup)
    wdn[...] = jnp.zeros_like(wdn)
    acc_q[...] = jnp.zeros_like(acc_q)
    acc_o[...] = jnp.zeros_like(acc_o)
    acc_u[...] = jnp.zeros_like(acc_u)
    acc_d[...] = jnp.zeros_like(acc_d)
    acc_b[...] = jnp.zeros_like(acc_b)
    acc_ub[...] = jnp.zeros_like(acc_ub)
    acc_qv[...] = jnp.zeros_like(acc_qv)
    lse[...] = jnp.zeros_like(lse)

    for b in range(count):
        seg = seg_ref[b : b + 1, :]
        doc = lax.broadcasted_iota(jnp.int32, (128, length), 0) - 64
        k_t = jnp.where((doc >= 0) & (seg == doc), 1.0, 0.0).astype(F32)
        q_t = jnp.where(
            (doc == 0) | ((doc > 0) & (seg != doc) & (seg != 0)), FAR, 0.0
        ).astype(F32)
        here = pl.ds(b * length, length)
        kext[here, :] = k_t.T.astype(BF16)
        qext[here, :] = q_t.T.astype(BF16)

    def gather(buf, group, cols, step):
        align = 8 if step % 8 == 0 else 1

        def one(p, _):
            at = pl.multiple_of(p * step, align)
            piece[pl.ds(at, step), 0:cols] = buf[group * per + p].astype(F32)
            return 0

        lax.fori_loop(0, per, one, 0)

    def take_qkv(g, _):
        gather(buf_a, g, 640, take)
        where = pl.ds(pl.multiple_of(inset(g), 64), 192)
        for part in range(3):
            wqkv[g, where, 256 * part : 256 * part + 192] = piece[
                0:192, 192 * part : 192 * part + 192
            ].astype(BF16)
        small[g] = piece[0:192, 512:640].T[64:80]
        return 0

    lax.fori_loop(0, GROUPS, take_qkv, 0)

    def take_rest(g, _):
        where = pl.ds(pl.multiple_of(inset(g), 64), 192)
        gather(buf_o, g, 768, take)
        wo[g, 0:192, :] = piece[0:192, 0:768].astype(BF16)
        gather(buf_u, g, 768, take)
        wup[g, where, :] = piece[0:192, 0:768].astype(BF16)
        gather(buf_d, g, 256, take_d)
        upb[g] = piece[0:768, 128:256].T[64:72]
        w = piece[0:768, 0:192].astype(BF16)

        @pl.when(g % 2 == 0)
        def _():
            wdn[g, :, 0:192] = w

        @pl.when(g % 2 == 1)
        def _():
            wdn[g, :, 64:256] = w

        return 0

    lax.fori_loop(0, GROUPS, take_rest, 0)
    rows_sm[...] = jnp.concatenate([small[g] for g in range(GROUPS)], -1)

    pad64 = jnp.zeros((1, 64), F32)

    def attend(g, b):
        here = pl.ds(pl.multiple_of(b * length, length), length)
        xw = x_ref[here, pl.ds(pl.multiple_of(edge(g), 128), 256)]
        bias = small[g]
        bq = jnp.concatenate([bias[0:1], pad64], -1)
        bv = jnp.concatenate([bias[1:2], pad64], -1)
        q = (dot(xw, wqkv[g, :, 0:256]) + bq).astype(BF16) * BF16(SCORE_SCALE)
        k = dot(xw, wqkv[g, :, 256:512]).astype(BF16)
        v = (dot(xw, wqkv[g, :, 512:768]) + bv).astype(BF16)
        qs[g, here, 0:128] = q[:, :128]
        qs[g, here, 128:256] = q[:, 128:] + qext[here, :]
        kk[g, here, 0:128] = k[:, :128]
        kk[g, here, 128:256] = k[:, 128:] + kext[here, :]
        vv[g, here, :] = v
        q = qs[g, here, :]
        k = kk[g, here, :]
        lanes = lane_ids((length, 128))
        out = jnp.zeros((length, 256), F32)
        for h in range(3):
            s = dot_nt(head_only(q, h, True), k)
            top = jnp.max(s, -1, keepdims=True)
            e = jnp.exp(s - top)
            total = jnp.sum(e, -1, keepdims=True)
            p = (e * (1.0 / total)).astype(BF16)
            out = out + dot(p, head_only(v, h))
            lse[here, :] = jnp.where(lanes == 3 * g + h, top + jnp.log(total), lse[here, :])
        ctx[g, here, :] = out.astype(BF16)

    def attend_step(i, _):
        attend(i // count, i % count)
        return 0

    lax.fori_loop(0, GROUPS * count, attend_step, 0)
    lse_t[...] = lse[...].T

    block = 256

    def ffn(i, _):
        here = pl.ds(pl.multiple_of(i * block, block), block)
        small_rows = rows_sm[...]
        b_out, b_n1, b_ff, b_n2 = (small_rows[j : j + 1] for j in (2, 3, 4, 5))
        gain1, gain2 = small_rows[6:7], small_rows[7:8]
        attn = dot(ctx[0, here, :], wo[0])
        for g in range(1, GROUPS):
            attn = attn + dot(ctx[g, here, :], wo[g])
        hidden1 = x_ref[here, :].astype(F32) + attn + b_out
        normed1, spread1 = normalize(hidden1)
        layer1 = normed1 * gain1 + b_n1
        low1 = layer1.astype(BF16)
        acts, slopes, outs = [], [], []
        for g in range(GROUPS):
            pre = dot(low1[:, edge(g) : edge(g) + 256], wup[g]) + upb[g, 0:1, :]
            act, slope = gelu_pair(pre)
            act = act.astype(BF16)
            acts.append(act)
            slopes.append(slope)
            outs.append(dot(act, wdn[g]))
        hidden2 = layer1 + spread_windows(outs) + b_ff
        normed2, spread2 = normalize(hidden2)
        lo_ref[here, :] = (normed2 * gain2 + b_n2).astype(BF16)
        cot = cot_ref[here, :].astype(F32)
        grad_h2 = norm_back(cot, gain2, normed2, spread2)
        low_f = grad_h2.astype(BF16)
        f_t = low_f.T
        l_t = low1.T
        backs = []
        for g in range(GROUPS):
            acc_d[g] += dot(f_t[192 * g : 192 * g + 192], acts[g])
            grad_act = dot_nt(low_f[:, edge(g) : edge(g) + 256], wdn[g])
            grad_pre = (grad_act * slopes[g]).astype(BF16)
            acc_ub[g, 0:1, :] += col_sum(grad_pre.astype(F32))
            acc_u[g] += dot(l_t[192 * g : 192 * g + 192], grad_pre)
            backs.append(dot_nt(grad_pre, wup[g]))
        grad_l1 = grad_h2 + spread_windows(backs)
        grad_h1 = norm_back(grad_l1, gain1, normed1, spread1)
        ig_ref[here, :] = grad_h1
        low_a = grad_h1.astype(BF16)
        for g in range(GROUPS):
            gctx[g, here, :] = dot_nt(low_a, wo[g]).astype(BF16)
            acc_o[g] += dot(ctx[g, here, :].T[0:192], low_a)
        acc_b[2:3] += col_sum(grad_h1)
        acc_b[3:4] += col_sum(grad_l1)
        acc_b[4:5] += col_sum(grad_h2)
        acc_b[5:6] += col_sum(cot)
        acc_b[6:7] += col_sum(grad_l1 * normed1)
        acc_b[7:8] += col_sum(cot * normed2)
        return 0

    lax.fori_loop(0, rows // block, ffn, 0)

    def attend_back(g, b):
        here = pl.ds(pl.multiple_of(b * length, length), length)
        q = qs[g, here, :]
        k = kk[g, here, :]
        v = vv[g, here, :]
        d_out = gctx[g, here, :]
        d_q = jnp.zeros((length, 256), F32)
        d_k = jnp.zeros((length, 256), F32)
        d_v = jnp.zeros((length, 256), F32)
        for h in range(3):
            s_t = dot_nt(k, head_only(q, h, True))
            p_t = jnp.exp(s_t - lse_t[pl.ds(3 * g + h, 1), here])
            d_h = head_only(d_out, h)
            dp_t = dot_nt(v, d_h)
            inner = col_sum(p_t * dp_t)
            ds_t = (p_t * (dp_t - inner)).astype(BF16)
            d_v = d_v + dot(p_t.astype(BF16), d_h)
            d_k = d_k + dot(ds_t, head_only(q, h))
            d_q = d_q + dot_tn(ds_t, head_only(k, h))
        low_q = (d_q * SCORE_SCALE).astype(BF16)
        low_v = d_v.astype(BF16)
        gm[here, 0:256] = low_q
        gm[here, 256:512] = d_k.astype(BF16)
        gm[here, 512:768] = low_v
        acc_qv[g, 0:1, :] += col_sum(low_q.astype(F32))
        acc_qv[g, 1:2, :] += col_sum(low_v.astype(F32))

    def back_step(g, _):
        for b in range(count):
            attend_back(g, b)
        mixed = gm[...]
        at = pl.ds(pl.multiple_of(edge(g), 128), 256)
        xw = x_ref[:, at]
        tmp_t[...] = dot(xw.T, mixed)
        acc_q[g] = tmp_t[pl.ds(pl.multiple_of(inset(g), 64), 192), :]
        ig_ref[:, at] += dot_nt(mixed, wqkv[g])
        return 0

    lax.fori_loop(0, GROUPS, back_step, 0)

    def scatter(buf, group, cols, step):
        align = 8 if step % 8 == 0 else 1

        def one(p, _):
            at = pl.multiple_of(p * step, align)
            buf[group * per + p] = piece[pl.ds(at, step), 0:cols].astype(buf.dtype)
            return 0

        lax.fori_loop(0, per, one, 0)

    for g in range(GROUPS):
        for part in range(3):
            piece[0:192, 192 * part : 192 * part + 192] = acc_q[g, :, 256 * part : 256 * part + 192]
        mine = jnp.concatenate(
            [acc_qv[g, 0:2, 0:192], acc_b[2:8, 192 * g : 192 * g + 192]], 0
        )
        high = mine.astype(BF16).astype(F32)
        side = jnp.concatenate([high, mine - high, jnp.zeros((112, 192), F32)], 0)
        piece[0:192, 576:640] = side.T[:, 0:64]
        scatter(ga_ref, g, 640, take)
        piece[0:192, 0:768] = acc_o[g]
        scatter(go_ref, g, 768, take)
        piece[0:192, 0:768] = acc_u[g]
        scatter(gu_ref, g, 768, take)
        ub = acc_ub[g, 0:1, :]
        high = ub.astype(BF16).astype(F32)
        full = jnp.concatenate([acc_d[g], high, ub - high, jnp.zeros((62, 768), F32)], 0)
        piece[0:768, 0:256] = full.T
        scatter(gd_ref, g, 256, take_d)


def layer(tokens, segment_ids, cotangent, buf_a, buf_o, buf_u, buf_d):
    count, length, width = tokens.shape
    rows = count * length
    grad = lambda buf: jax.ShapeDtypeStruct(buf.shape, BF16)
    scratch = [
        pltpu.VMEM((768, 768), F32),
        pltpu.VMEM((4, 256, 768), BF16),
        pltpu.VMEM((4, 256, 768), BF16),
        pltpu.VMEM((4, 256, 768), BF16),
        pltpu.VMEM((4, 768, 256), BF16),
        pltpu.VMEM((4, 16, 192), F32),
        pltpu.VMEM((16, 768), F32),
        pltpu.VMEM((4, 8, 768), F32),
        pltpu.VMEM((rows, 128), BF16),
        pltpu.VMEM((rows, 128), BF16),
        pltpu.VMEM((4, rows, 256), BF16),
        pltpu.VMEM((4, rows, 256), BF16),
        pltpu.VMEM((4, rows, 256), BF16),
        pltpu.VMEM((4, rows, 256), BF16),
        pltpu.VMEM((4, rows, 256), BF16),
        pltpu.VMEM((rows, 768), BF16),
        pltpu.VMEM((rows, 128), F32),
        pltpu.VMEM((128, rows), F32),
        pltpu.VMEM((4, 192, 768), F32),
        pltpu.VMEM((4, 192, 768), F32),
        pltpu.VMEM((4, 192, 768), F32),
        pltpu.VMEM((4, 192, 768), F32),
        pltpu.VMEM((8, 768), F32),
        pltpu.VMEM((4, 8, 768), F32),
        pltpu.VMEM((4, 8, 256), F32),
        pltpu.VMEM((256, 768), F32),
    ]
    vm = pl.BlockSpec(memory_space=pltpu.VMEM)
    return pl.pallas_call(
        body,
        out_shape=(
            jax.ShapeDtypeStruct((rows, width), BF16),
            jax.ShapeDtypeStruct((rows, width), F32),
            grad(buf_a), grad(buf_o), grad(buf_u), grad(buf_d),
        ),
        in_specs=[vm] * 7,
        out_specs=[vm] * 6,
        scratch_shapes=scratch,
        compiler_params=pltpu.CompilerParams(vmem_limit_bytes=62 * 1024 * 1024),
    )(tokens.reshape(rows, width), segment_ids, cotangent.reshape(rows, width), buf_a, buf_o, buf_u, buf_d)


def local(tokens, segment_ids, qkv_weight, out_weight, up_weight, down_weight, biases, up_bias, gains, cotangent):
    axes = ("dp", "fsdp")
    take, take_d = qkv_weight.shape[0], down_weight.shape[0]
    zeros = lambda r, c: jnp.zeros((r, c), BF16)
    pack_a = jnp.concatenate([qkv_weight, biases.T, gains.T, zeros(take, 56)], 1)
    pack_d = jnp.concatenate([down_weight, up_bias[:, None], zeros(take_d, 63)], 1)
    gather = lambda v: lax.all_gather(v, axes, axis=0, tiled=True).reshape(32, -1, v.shape[1])
    out, ig, ga, go, gu, gd = layer(
        tokens, segment_ids, cotangent, gather(pack_a), gather(out_weight), gather(up_weight), gather(pack_d)
    )
    total = lambda v: lax.psum_scatter(
        v.reshape(-1, v.shape[2]).astype(F32), axes, scatter_dimension=0, tiled=True
    )
    ga, go, gu, gd = total(ga), total(go), total(gu), total(gd)
    side = (ga[:, 576:584] + ga[:, 584:592]).T
    return (
        out.reshape(tokens.shape), ig.reshape(tokens.shape),
        ga[:, :576], go, gu, gd[:, :192], side[:6], gd[:, 192] + gd[:, 193], side[6:8],
    )


def solution(mesh):
    row, col = P(("dp", "fsdp")), P(None, ("dp", "fsdp"))
    in_specs = (row, row, row, row, row, row, col, row, col, row)
    out_specs = (row, row, row, row, row, row, col, row, col)
    return jax.shard_map(local, mesh=mesh, in_specs=in_specs, out_specs=out_specs, check_vma=False)
```

```python
from functools import partial

import jax
import jax.numpy as jnp
from jax import lax
from jax.experimental import pallas as pl
from jax.experimental.pallas import tpu as pltpu
from jax.sharding import PartitionSpec as P

HEADS = 12
GROUPS = 4
EPSILON = 1e-05
SCORE_SCALE = 0.125
FAR = -1e30
F32 = jnp.float32
BF16 = jnp.bfloat16
ERF_P = 0.39
ERF_C = (
    0.23532515472880694, 0.09138881837358971, 0.6495583919191722,
    -0.6353990321145604, 0.8866636029850097, -0.22753693758818713,
)
MESH = pl.DeviceIdType.MESH
NT = (((1,), (1,)), ((), ()))
TN = (((0,), (0,)), ((), ()))


def dot(a, b):
    return jnp.dot(a, b, preferred_element_type=F32)


def dot_nt(a, b):
    return lax.dot_general(a, b, NT, preferred_element_type=F32)


def dot_tn(a, b):
    return lax.dot_general(a, b, TN, preferred_element_type=F32)


def edge(group):
    return (group // 2) * 384 + (group % 2) * 128


def inset(group):
    return (group % 2) * 64


def aligned(value, step):
    return value if isinstance(value, int) else pl.multiple_of(value, step)


def lane_ids(shape):
    return lax.broadcasted_iota(jnp.int32, shape, len(shape) - 1)


def head_only(block, head, extra=False):
    lanes = lane_ids(block.shape)
    keep = (lanes >= 64 * head) & (lanes < 64 * head + 64)
    if extra:
        keep = keep | (lanes >= 192)
    return jnp.where(keep, block, jnp.zeros_like(block))


def gelu_pair(v):
    a = jnp.abs(v)
    u = jnp.exp(v * v * (-0.5))
    t = 1.0 / (1.0 + a * (ERF_P * 0.7071067811865476))
    h = ERF_C[5] * 0.5
    for c in ERF_C[4::-1]:
        h = h * t + 0.5 * c
    h = h * t * u
    phi = jnp.where(v >= 0, 1.0 - h, h)
    return v * phi, phi + v * u * 0.3989422804014327


def normalize(hidden):
    centre = hidden - jnp.mean(hidden, -1, keepdims=True)
    spread = lax.rsqrt(jnp.mean(centre * centre, -1, keepdims=True) + EPSILON)
    return centre * spread, spread


def norm_back(upstream, gain, normed, spread):
    scaled = upstream * gain
    return spread * (
        scaled
        - jnp.mean(scaled, -1, keepdims=True)
        - normed * jnp.mean(scaled * normed, -1, keepdims=True)
    )


def spread_windows(parts):
    tiles = []
    for pair in range(2):
        low, high = parts[2 * pair], parts[2 * pair + 1]
        tiles += [low[:, :128], low[:, 128:] + high[:, :128], high[:, 128:]]
    return jnp.concatenate(tiles, -1)


def col_sum(v):
    return jnp.sum(v, 0, keepdims=True)


class Links:
    def __init__(self):
        dp, fsdp = lax.axis_index("dp"), lax.axis_index("fsdp")
        self.at = {"x": dp // 2, "c": dp % 2, "z": fsdp // 2, "y": fsdp % 2}
        self.dp, self.fsdp = dp, fsdp

    def shifted(self, dim, by=1):
        size = 4 if dim == "z" else 2
        place = dict(self.at)
        place[dim] = (place[dim] + by) % size
        return place

    def device(self, place):
        return (place["x"] * 2 + place["c"], place["z"] * 2 + place["y"])

    def partner(self, dim, by=1):
        return self.device(self.shifted(dim, by))

    def greet(self):
        barrier = pltpu.get_barrier_semaphore()
        others = [self.partner("x"), self.partner("c")]
        others += [(self.dp, (self.fsdp + j) % 8) for j in range(1, 8)]
        for other in others:
            pl.semaphore_signal(barrier, inc=1, device_id=other, device_id_type=MESH)

    def meet(self):
        pl.semaphore_wait(pltpu.get_barrier_semaphore(), 9)


def remote(src, dst, sems, slot, device):
    return pltpu.make_async_remote_copy(
        src_ref=src, dst_ref=dst, send_sem=sems[0].at[slot], recv_sem=sems[1].at[slot],
        device_id=device, device_id_type=MESH,
    )


class Gather:
    def __init__(self, links, buf, second, third, sems):
        self.links, self.buf, self.sems = links, buf, sems
        self.second, self.third = second, third

    def slot(self, place):
        return place["c"] * 16 + place[self.third] * 8 + place[self.second] * 4 + place["z"]

    def run(self, place, level):
        slot = self.slot(place)
        size = (1, 4, 8)[level]
        return self.buf.at[pl.ds(slot - slot % size, size)]

    def hop(self, n, theirs):
        links = self.links
        here = links.at
        if n < 3:
            j = n + 1
            other, back = links.shifted("z", j), links.shifted("z", 4 - j)
            level = 0
        elif n < 5:
            other = back = links.shifted((self.second, self.third)[n - 3])
            level = n - 2
        else:
            other = back = links.shifted("c")
            if n == 5:
                level = 1
            else:
                level = n - 5
                dim = (self.second, self.third)[n - 6]
                here = links.shifted(dim)
                back = dict(back)
                back[dim] = here[dim]
        run = self.run(back if theirs else here, level)
        return remote(run, run, self.sems, n, links.device(other))

    def start(self, *stages):
        for n in stages:
            self.hop(n, False).start()

    def arrive(self, *stages):
        for n in stages:
            self.hop(n, True).wait_recv()

    def finish(self):
        for n in range(8):
            self.hop(n, False).wait_send()


class Reduce:
    def __init__(self, links, buf, land, second, third, sems):
        self.links, self.buf, self.land, self.sems = links, buf, land, sems
        self.second, self.third = second, third
        at = links.at
        self.base = (
            0, at["c"] * 16, at["c"] * 16 + at[third] * 8,
            at["c"] * 16 + at[third] * 8 + at[second] * 4,
        )

    def hop(self, n):
        links = self.links
        if n < 3:
            dim = ("c", self.third, self.second)[n]
            size, place = (16, 8, 4)[n], (0, 16, 24)[n]
            start = self.base[n] + (1 - links.at[dim]) * size
            other = links.partner(dim)
        else:
            j = n - 2
            size, place = 1, 25 + n
            start = self.base[3] + (links.at["z"] + j) % 4
            other = links.partner("z", j)
        return remote(
            self.buf.at[pl.ds(start, size)], self.land.at[pl.ds(place, size)], self.sems, n, other
        )

    def start(self, *stages):
        for n in stages:
            self.hop(n).start()

    def arrive(self, *stages):
        for n in stages:
            self.hop(n).wait_recv()

    def add(self, n):
        size, place = (16, 8, 4)[n], (0, 16, 24)[n]
        start = self.base[n + 1]

        def one(k, _):
            total = self.buf[start + k].astype(F32) + self.land[place + k].astype(F32)
            self.buf[start + k] = total.astype(BF16)
            return 0

        lax.fori_loop(0, size, one, 0)

    def result(self):
        total = self.buf[self.base[3] + self.links.at["z"]].astype(F32)
        for k in range(28, 31):
            total = total + self.land[k].astype(F32)
        return total

    def finish(self):
        for n in range(6):
            self.hop(n).wait_send()


def body(linked, *refs):
    x_ref, seg_ref, cot_ref = refs[:3]
    in_a, in_o, in_u, in_d = refs[3:7]
    lo_ref, ig_ref, ga_ref, go_ref, gu_ref, gd_ref = refs[7:13]
    (
        piece, wqkv, wo, wup, wdn, small, rows_sm, upb,
        qext, kext, qs, kk, vv, ctx, gctx, gm, lse, lse_t,
        acc_o, acc_u, acc_d, acc_b, acc_ub, acc_qv, tmp_t,
    ) = refs[13:38]
    count, length = seg_ref.shape
    rows, width = x_ref.shape
    if linked:
        buf_a, buf_o, buf_u, buf_d, land_a, land_o, land_u, land_d = refs[38:46]
        sems = refs[46:]
        links = Links()
        links.greet()
        gather_o = Gather(links, buf_o, "x", "y", sems[2:4])
        gather_u = Gather(links, buf_u, "y", "x", sems[4:6])
        gather_d = Gather(links, buf_d, "x", "y", sems[6:8])
        reduce_o = Reduce(links, buf_o, land_o, "x", "y", sems[8:10])
        reduce_u = Reduce(links, buf_u, land_u, "y", "x", sems[10:12])
        reduce_d = Reduce(links, buf_d, land_d, "x", "y", sems[12:14])
        gathers, reduces = (gather_o, gather_u, gather_d), (reduce_o, reduce_u, reduce_d)
        out_a, out_o, out_u, out_d = buf_a, buf_o, buf_u, buf_d
    else:
        buf_a, buf_o, buf_u, buf_d = in_a, in_o, in_u, in_d
        out_a, out_o, out_u, out_d = ga_ref, go_ref, gu_ref, gd_ref
    n_dev, take, _ = buf_a.shape
    per = n_dev // GROUPS
    take_d = buf_d.shape[1]

    def group_of(j):
        if not linked:
            return j
        return ((links.at["x"] + j // 2) % 2) * 2 + (links.at["c"] + j % 2) % 2

    def slot_of(second, g, p):
        if not linked:
            return g * per + p
        x, c, z, y = g // 2, g % 2, p // 2, p % 2
        if second == "x":
            return c * 16 + y * 8 + x * 4 + z
        return c * 16 + x * 8 + y * 4 + z

    wqkv[...] = jnp.zeros_like(wqkv)
    wup[...] = jnp.zeros_like(wup)
    wdn[...] = jnp.zeros_like(wdn)
    wo[...] = jnp.zeros_like(wo)
    acc_o[...] = jnp.zeros_like(acc_o)
    acc_u[...] = jnp.zeros_like(acc_u)
    acc_d[...] = jnp.zeros_like(acc_d)
    acc_b[...] = jnp.zeros_like(acc_b)
    acc_ub[...] = jnp.zeros_like(acc_ub)
    acc_qv[...] = jnp.zeros_like(acc_qv)
    lse[...] = jnp.zeros_like(lse)

    for b in range(count):
        seg = seg_ref[b : b + 1, :]
        doc = lax.broadcasted_iota(jnp.int32, (128, length), 0) - 64
        k_t = jnp.where((doc >= 0) & (seg == doc), 1.0, 0.0).astype(F32)
        q_t = jnp.where(
            (doc == 0) | ((doc > 0) & (seg != doc) & (seg != 0)), FAR, 0.0
        ).astype(F32)
        here = pl.ds(b * length, length)
        kext[here, :] = k_t.T.astype(BF16)
        qext[here, :] = q_t.T.astype(BF16)

    if linked:
        buf_a[links.dp * 8 + links.fsdp] = in_a[...]
        for one, ref in zip(gathers, (in_o, in_u, in_d)):
            one.buf[one.slot(links.at)] = ref[...]

        def near_a(j, theirs):
            other, back = (links.fsdp + j) % 8, (links.fsdp + 8 - j) % 8
            run = buf_a.at[pl.ds(links.dp * 8 + (back if theirs else links.fsdp), 1)]
            return remote(run, run, sems[0:2], j - 1, (links.dp, back if theirs else other))

        def far_a(kind, theirs):
            x, c = links.at["x"], links.at["c"]
            dim = ("c", "x", "c")[kind]
            sent = (x if kind < 2 else 1 - x) * 2 + c
            got = ((x * 2 + 1 - c), ((1 - x) * 2 + c), ((1 - x) * 2 + 1 - c))[kind]
            run = buf_a.at[pl.ds((got if theirs else sent) * 8, 8)]
            return remote(run, run, sems[0:2], 7 + kind, links.partner(dim))

        links.meet()
        for j in range(1, 8):
            near_a(j, False).start()
        gather_o.start(0, 1, 2)
        for j in range(1, 8):
            near_a(j, True).wait_recv()
        far_a(0, False).start()
        far_a(1, False).start()

    def gather(buf, second, group, cols, step):
        def one(p, _):
            at = pl.multiple_of(p * step, 8)
            slot = group * per + p if second is None else slot_of(second, group, p)
            piece[pl.ds(at, step), 0:cols] = buf[slot].astype(F32)
            return 0

        lax.fori_loop(0, per, one, 0)

    def take_qkv(g):
        gather(buf_a, None, g, 640, take)
        where = pl.ds(pl.multiple_of(inset(g), 64), 192)
        for part in range(3):
            wqkv[g, where, 256 * part : 256 * part + 192] = piece[
                0:192, 192 * part : 192 * part + 192
            ].astype(BF16)
        small[g] = piece[0:192, 512:640].T[64:80]

    def take_rest(g, _):
        where = pl.ds(pl.multiple_of(inset(g), 64), 192)
        gather(buf_o, "x", g, 768, take)
        wo[g, 0:192, :] = piece[0:192, 0:768].astype(BF16)
        gather(buf_u, "y", g, 768, take)
        wup[g, where, :] = piece[0:192, 0:768].astype(BF16)
        gather(buf_d, "x", g, 256, take_d)
        upb[g] = piece[0:768, 128:256].T[64:72]
        w = piece[0:768, 0:192].astype(BF16)

        @pl.when(g % 2 == 0)
        def _():
            wdn[g, :, 0:192] = w

        @pl.when(g % 2 == 1)
        def _():
            wdn[g, :, 64:256] = w

        return 0

    pad64 = jnp.zeros((1, 64), F32)

    def attend(g, b):
        here = pl.ds(pl.multiple_of(b * length, length), length)
        xw = x_ref[here, pl.ds(pl.multiple_of(edge(g), 128), 256)]
        bias = small[g]
        bq = jnp.concatenate([bias[0:1], pad64], -1)
        bv = jnp.concatenate([bias[1:2], pad64], -1)
        q = (dot(xw, wqkv[g, :, 0:256]) + bq).astype(BF16) * BF16(SCORE_SCALE)
        k = dot(xw, wqkv[g, :, 256:512]).astype(BF16)
        v = (dot(xw, wqkv[g, :, 512:768]) + bv).astype(BF16)
        qs[g, here, 0:128] = q[:, :128]
        qs[g, here, 128:256] = q[:, 128:] + qext[here, :]
        kk[g, here, 0:128] = k[:, :128]
        kk[g, here, 128:256] = k[:, 128:] + kext[here, :]
        vv[g, here, :] = v
        q = qs[g, here, :]
        k = kk[g, here, :]
        lanes = lane_ids((length, 128))
        out = jnp.zeros((length, 256), F32)
        for h in range(3):
            s = dot_nt(head_only(q, h, True), k)
            top = jnp.max(s, -1, keepdims=True)
            e = jnp.exp(s - top)
            total = jnp.sum(e, -1, keepdims=True)
            p = (e * (1.0 / total)).astype(BF16)
            out = out + dot(p, head_only(v, h))
            lse[here, :] = jnp.where(lanes == 3 * g + h, top + jnp.log(total), lse[here, :])
        ctx[g, here, :] = out.astype(BF16)

    def attend_step(i, _):
        g = group_of(i // count)

        if linked:

            @pl.when(i == count)
            def _():
                far_a(0, True).wait_recv()

            @pl.when(i == 2 * count)
            def _():
                far_a(1, True).wait_recv()
                far_a(2, False).start()

            @pl.when(i == 3 * count)
            def _():
                far_a(2, True).wait_recv()

        @pl.when(i % count == 0)
        def _():
            take_qkv(g)

        attend(g, i % count)

        if linked:

            @pl.when(i == 0)
            def _():
                gather_o.arrive(0, 1, 2)
                gather_o.start(3, 5)
                gather_u.start(0, 1, 2)
                gather_d.start(0, 1, 2)

            @pl.when(i == 2)
            def _():
                gather_u.arrive(0, 1, 2)
                gather_u.start(3, 5)
                gather_d.arrive(0, 1, 2)
                gather_d.start(3, 5)
                gather_o.arrive(3)
                gather_o.start(4, 6)

            @pl.when(i == 4)
            def _():
                gather_u.arrive(3)
                gather_u.start(4, 6)
                gather_d.arrive(3)
                gather_d.start(4, 6)

            @pl.when(i == 5)
            def _():
                gather_o.arrive(4)
                gather_o.start(7)

            @pl.when(i == 6)
            def _():
                gather_u.arrive(4)
                gather_u.start(7)
                gather_d.arrive(4)
                gather_d.start(7)

        return 0

    lax.fori_loop(0, GROUPS * count, attend_step, 0)
    lse_t[...] = lse[...].T
    if linked:
        for one in gathers:
            one.arrive(5, 6, 7)
            one.finish()
        for j in range(1, 8):
            near_a(j, False).wait_send()
        for kind in range(3):
            far_a(kind, False).wait_send()
    lax.fori_loop(0, GROUPS, take_rest, 0)
    rows_sm[...] = jnp.concatenate([small[g] for g in range(GROUPS)], -1)

    block = 256

    def ffn(i, _):
        here = pl.ds(pl.multiple_of(i * block, block), block)
        small_rows = rows_sm[...]
        b_out, b_n1, b_ff, b_n2 = (small_rows[j : j + 1] for j in (2, 3, 4, 5))
        gain1, gain2 = small_rows[6:7], small_rows[7:8]
        attn = dot(ctx[0, here, :], wo[0])
        for g in range(1, GROUPS):
            attn = attn + dot(ctx[g, here, :], wo[g])
        hidden1 = x_ref[here, :].astype(F32) + attn + b_out
        normed1, spread1 = normalize(hidden1)
        layer1 = normed1 * gain1 + b_n1
        low1 = layer1.astype(BF16)
        acts, slopes, outs = [], [], []
        for g in range(GROUPS):
            pre = dot(low1[:, edge(g) : edge(g) + 256], wup[g]) + upb[g, 0:1, :]
            act, slope = gelu_pair(pre)
            act = act.astype(BF16)
            acts.append(act)
            slopes.append(slope)
            outs.append(dot(act, wdn[g]))
        hidden2 = layer1 + spread_windows(outs) + b_ff
        normed2, spread2 = normalize(hidden2)
        lo_ref[here, :] = (normed2 * gain2 + b_n2).astype(BF16)
        cot = cot_ref[here, :].astype(F32)
        grad_h2 = norm_back(cot, gain2, normed2, spread2)
        low_f = grad_h2.astype(BF16)
        f_t = low_f.T
        l_t = low1.T
        backs = []
        for g in range(GROUPS):
            acc_d[g] += dot(f_t[192 * g : 192 * g + 192], acts[g])
            grad_act = dot_nt(low_f[:, edge(g) : edge(g) + 256], wdn[g])
            grad_pre = (grad_act * slopes[g]).astype(BF16)
            acc_ub[g, 0:1, :] += col_sum(grad_pre.astype(F32))
            acc_u[g] += dot(l_t[192 * g : 192 * g + 192], grad_pre)
            backs.append(dot_nt(grad_pre, wup[g]))
        grad_l1 = grad_h2 + spread_windows(backs)
        grad_h1 = norm_back(grad_l1, gain1, normed1, spread1)
        ig_ref[here, :] = grad_h1
        low_a = grad_h1.astype(BF16)
        for g in range(GROUPS):
            gctx[g, here, :] = dot_nt(low_a, wo[g]).astype(BF16)
            acc_o[g] += dot(ctx[g, here, :].T[0:192], low_a)
        acc_b[2:3] += col_sum(grad_h1)
        acc_b[3:4] += col_sum(grad_l1)
        acc_b[4:5] += col_sum(grad_h2)
        acc_b[5:6] += col_sum(cot)
        acc_b[6:7] += col_sum(grad_l1 * normed1)
        acc_b[7:8] += col_sum(cot * normed2)
        return 0

    lax.fori_loop(0, rows // block, ffn, 0)

    def scatter(buf, second, group, cols, step):
        def one(p, _):
            at = pl.multiple_of(p * step, 8)
            slot = group * per + p if second is None else slot_of(second, group, p)
            buf[slot] = piece[pl.ds(at, step), 0:cols].astype(BF16)
            return 0

        lax.fori_loop(0, per, one, 0)

    def give_rest(g, _):
        piece[0:192, 0:768] = acc_o[g]
        scatter(out_o, "x", g, 768, take)
        piece[0:192, 0:768] = acc_u[g]
        scatter(out_u, "y", g, 768, take)
        ub = acc_ub[g, 0:1, :]
        high = ub.astype(BF16).astype(F32)
        full = jnp.concatenate([acc_d[g], high, ub - high, jnp.zeros((62, 768), F32)], 0)
        piece[0:768, 0:256] = full.T
        scatter(out_d, "x", g, 256, take_d)
        return 0

    lax.fori_loop(0, GROUPS, give_rest, 0)
    if linked:
        for one in reduces:
            one.start(0)
    for g in range(GROUPS):
        small[g, 0:8] = acc_b[0:8, 192 * g : 192 * g + 192]

    def attend_back(g, b):
        here = pl.ds(pl.multiple_of(b * length, length), length)
        q = qs[g, here, :]
        k = kk[g, here, :]
        v = vv[g, here, :]
        d_out = gctx[g, here, :]
        d_q = jnp.zeros((length, 256), F32)
        d_k = jnp.zeros((length, 256), F32)
        d_v = jnp.zeros((length, 256), F32)
        for h in range(3):
            s_t = dot_nt(k, head_only(q, h, True))
            p_t = jnp.exp(s_t - lse_t[pl.ds(3 * g + h, 1), here])
            d_h = head_only(d_out, h)
            dp_t = dot_nt(v, d_h)
            inner = col_sum(p_t * dp_t)
            ds_t = (p_t * (dp_t - inner)).astype(BF16)
            d_v = d_v + dot(p_t.astype(BF16), d_h)
            d_k = d_k + dot(ds_t, head_only(q, h))
            d_q = d_q + dot_tn(ds_t, head_only(k, h))
        low_q = (d_q * SCORE_SCALE).astype(BF16)
        low_v = d_v.astype(BF16)
        gm[here, 0:256] = low_q
        gm[here, 256:512] = d_k.astype(BF16)
        gm[here, 512:768] = low_v
        acc_qv[g, 0:1, :] += col_sum(low_q.astype(F32))
        acc_qv[g, 1:2, :] += col_sum(low_v.astype(F32))

    if linked:

        def back_a(kind):
            x, c = links.at["x"], links.at["c"]
            sent = ((1 - x) * 2 + 1 - c, (1 - x) * 2 + c, x * 2 + 1 - c)[kind]
            return remote(
                buf_a.at[pl.ds(sent * 8, 8)], land_a.at[pl.ds(8 * kind, 8)],
                sems[14:16], kind, links.partner(("c", "x", "c")[kind]),
            )

        def home_a(j):
            other = (links.fsdp + j) % 8
            return remote(
                buf_a.at[pl.ds(links.dp * 8 + other, 1)], land_a.at[pl.ds(23 + j, 1)],
                sems[14:16], 2 + j, (links.dp, other),
            )

        def join_a(g, first):
            def one(p, _):
                total = buf_a[g * per + p].astype(F32) + land_a[first + p].astype(F32)
                buf_a[g * per + p] = total.astype(BF16)
                return 0

            lax.fori_loop(0, per, one, 0)

    def back_step(i, _):
        j = GROUPS - 1 - i
        g = group_of(j)
        attend_back(g, 0)

        if linked:

            @pl.when(i == 2)
            def _():
                for one in reduces:
                    one.arrive(1)
                    one.add(1)
                    one.start(2)

        for b in range(1, count):
            attend_back(g, b)
        mixed = gm[...]
        at = pl.ds(pl.multiple_of(edge(g), 128), 256)
        xw = x_ref[:, at]
        tmp_t[...] = dot(xw.T, mixed)
        ig_ref[:, at] += dot_nt(mixed, wqkv[g])
        where = pl.ds(pl.multiple_of(inset(g), 64), 192)
        for part in range(3):
            piece[0:192, 192 * part : 192 * part + 192] = tmp_t[where, 256 * part : 256 * part + 192]
        mine = jnp.concatenate([acc_qv[g, 0:2, 0:192], small[g, 2:8]], 0)
        high = mine.astype(BF16).astype(F32)
        side = jnp.concatenate([high, mine - high, jnp.zeros((112, 192), F32)], 0)
        piece[0:192, 576:640] = side.T[:, 0:64]
        scatter(out_a, None, g, 640, take)

        if linked:

            @pl.when(i == 0)
            def _():
                back_a(0).start()
                for one in reduces:
                    one.arrive(0)
                    one.add(0)
                    one.start(1)

            @pl.when(i == 1)
            def _():
                back_a(0).wait_recv()
                join_a(g, 0)
                back_a(1).start()

            @pl.when(i == 2)
            def _():
                back_a(2).start()
                for one in reduces:
                    one.arrive(2)
                    one.add(2)
                    one.start(3, 4, 5)

            @pl.when(i == 3)
            def _():
                back_a(1).wait_recv()
                back_a(2).wait_recv()
                join_a(g, 8)
                join_a(g, 16)
                for k in range(1, 8):
                    home_a(k).start()

        return 0

    lax.fori_loop(0, GROUPS, back_step, 0)
    if linked:
        for one, ref in zip(reduces, (go_ref, gu_ref, gd_ref)):
            one.arrive(3, 4, 5)
            ref[...] = one.result()
            one.finish()
        for k in range(3):
            back_a(k).wait_send()
        total = buf_a[links.dp * 8 + links.fsdp].astype(F32)
        for k in range(1, 8):
            home_a(k).wait_recv()
            total = total + land_a[23 + k].astype(F32)
        ga_ref[...] = total
        for k in range(1, 8):
            home_a(k).wait_send()


def layer(linked, tokens, segment_ids, cotangent, a, o, u, d):
    count, length, width = tokens.shape
    rows = count * length
    kind = F32 if linked else BF16
    scratch = [
        pltpu.VMEM((768, 768), F32),
        pltpu.VMEM((4, 256, 768), BF16),
        pltpu.VMEM((4, 256, 768), BF16),
        pltpu.VMEM((4, 256, 768), BF16),
        pltpu.VMEM((4, 768, 256), BF16),
        pltpu.VMEM((4, 16, 192), F32),
        pltpu.VMEM((16, 768), F32),
        pltpu.VMEM((4, 8, 768), F32),
        pltpu.VMEM((rows, 128), BF16),
        pltpu.VMEM((rows, 128), BF16),
        pltpu.VMEM((4, rows, 256), BF16),
        pltpu.VMEM((4, rows, 256), BF16),
        pltpu.VMEM((4, rows, 256), BF16),
        pltpu.VMEM((4, rows, 256), BF16),
        pltpu.VMEM((4, rows, 256), BF16),
        pltpu.VMEM((rows, 768), BF16),
        pltpu.VMEM((rows, 128), F32),
        pltpu.VMEM((128, rows), F32),
        pltpu.VMEM((4, 192, 768), F32),
        pltpu.VMEM((4, 192, 768), F32),
        pltpu.VMEM((4, 192, 768), F32),
        pltpu.VMEM((8, 768), F32),
        pltpu.VMEM((4, 8, 768), F32),
        pltpu.VMEM((4, 8, 256), F32),
        pltpu.VMEM((256, 768), F32),
    ]
    params = {"vmem_limit_bytes": 62 * 1024 * 1024}
    if linked:
        scratch += [pltpu.VMEM((32,) + v.shape, BF16) for v in (a, o, u, d)]
        scratch += [pltpu.VMEM((31,) + v.shape, BF16) for v in (a, o, u, d)]
        for n in (10, 8, 8, 8, 6, 6, 6, 10):
            scratch += [pltpu.SemaphoreType.DMA((n,)), pltpu.SemaphoreType.DMA((n,))]
        params |= {"collective_id": 0, "has_side_effects": True}
    vm = pl.BlockSpec(memory_space=pltpu.VMEM)
    return pl.pallas_call(
        partial(body, linked),
        out_shape=(
            jax.ShapeDtypeStruct((rows, width), BF16),
            jax.ShapeDtypeStruct((rows, width), F32),
            *(jax.ShapeDtypeStruct(v.shape, kind) for v in (a, o, u, d)),
        ),
        in_specs=[vm] * 7,
        out_specs=[vm] * 6,
        scratch_shapes=scratch,
        compiler_params=pltpu.CompilerParams(**params),
    )(tokens.reshape(rows, width), segment_ids, cotangent.reshape(rows, width), a, o, u, d)


def local(
    linked, tokens, segment_ids, qkv_weight, out_weight, up_weight, down_weight,
    biases, up_bias, gains, cotangent,
):
    axes = ("dp", "fsdp")
    take, take_d = qkv_weight.shape[0], down_weight.shape[0]
    zeros = lambda r, c: jnp.zeros((r, c), BF16)
    pack_a = jnp.concatenate([qkv_weight, biases.T, gains.T, zeros(take, 56)], 1)
    pack_d = jnp.concatenate([down_weight, up_bias[:, None], zeros(take_d, 63)], 1)
    shards = (pack_a, out_weight, up_weight, pack_d)
    if not linked:
        shards = [
            lax.all_gather(v, axes, axis=0, tiled=True).reshape(32, -1, v.shape[1]) for v in shards
        ]
    out, ig, *grads = layer(linked, tokens, segment_ids, cotangent, *shards)
    if not linked:
        grads = [
            lax.psum_scatter(
                v.reshape(-1, v.shape[2]).astype(F32), axes, scatter_dimension=0, tiled=True
            )
            for v in grads
        ]
    ga, go, gu, gd = grads
    side = (ga[:, 576:584] + ga[:, 584:592]).T
    return (
        out.reshape(tokens.shape), ig.reshape(tokens.shape),
        ga[:, :576], go, gu, gd[:, :192], side[:6], gd[:, 192] + gd[:, 193], side[6:8],
    )


def solution(mesh):
    row, col = P(("dp", "fsdp")), P(None, ("dp", "fsdp"))
    in_specs = (row, row, row, row, row, row, col, row, col, row)
    out_specs = (row, row, row, row, row, row, col, row, col)
    linked = (mesh.shape["dp"], mesh.shape["fsdp"]) == (4, 8)
    return jax.shard_map(
        partial(local, linked), mesh=mesh, in_specs=in_specs, out_specs=out_specs, check_vma=False
    )
```
